32 devices in a mesh: fsdp: 2 (over y), ctx: 4 (over z), tp: 4 (over x, core).
Axes of the slice: x: 2, y: 2, z: 4, core: 2. Of those that a mesh axis runs over, the one named last changes fastest.
Arguments:
- tokens: bfloat16 [2, 4096, 1024], P('fsdp', 'ctx'), may hold values from -6 to 6
- cotangent: bfloat16 [2, 4096, 1024], P('fsdp', 'ctx'), may hold values from -6 to 6
- segment_ids: int32 [2, 4096], P('fsdp', 'ctx'), may hold values from 0 to 31, never falling along the last dimension, each value on 1 to 2048 neighbouring positions
- in_weight: bfloat16 [1024, 3, 1024], P('fsdp', None, 'tp'), may hold values from -0.25 to 0.25
- out_weight: bfloat16 [1024, 1024], P(('tp', 'fsdp')), may hold values from -0.5 to 0.5
- up_weight: bfloat16 [1024, 4096], P('fsdp', 'tp'), may hold values from -0.1875 to 0.1875
- down_weight: bfloat16 [4096, 1024], P(('tp', 'fsdp')), may hold values from -0.09375 to 0.09375
- query_bias: bfloat16 [1024], P(('tp', 'fsdp')), may hold values from -3 to 3
- value_bias: bfloat16 [1024], P(('tp', 'fsdp')), may hold values from -3 to 3
- out_bias: bfloat16 [1024], P('fsdp'), may hold values from -3 to 3
- up_bias: bfloat16 [4096], P(('tp', 'fsdp')), may hold values from -3 to 3
- down_bias: bfloat16 [1024], P('fsdp'), may hold values from -3 to 3
- first_gain: bfloat16 [1024], P('fsdp'), may hold values from 0.5 to 1.5
- first_shift: bfloat16 [1024], P('fsdp'), may hold values from -2 to 2
- second_gain: bfloat16 [1024], P('fsdp'), may hold values from 0.5 to 1.5
- second_shift: bfloat16 [1024], P('fsdp'), may hold values from -2 to 2
Outputs:
- activations: bfloat16 [2, 4096, 1024], P('fsdp', 'ctx')
- input_grad: float32 [2, 4096, 1024], P('fsdp', 'ctx')
- grad_in_weight: float32 [1024, 3, 1024], P('fsdp', None, 'tp')
- grad_out_weight: float32 [1024, 1024], P(('tp', 'fsdp'))
- grad_up_weight: float32 [1024, 4096], P('fsdp', 'tp')
- grad_down_weight: float32 [4096, 1024], P(('tp', 'fsdp'))
- grad_query_bias: float32 [1024], P(('tp', 'fsdp'))
- grad_value_bias: float32 [1024], P(('tp', 'fsdp'))
- grad_out_bias: float32 [1024], P('fsdp')
- grad_up_bias: float32 [4096], P(('tp', 'fsdp'))
- grad_down_bias: float32 [1024], P('fsdp')
- grad_first_gain: float32 [1024], P('fsdp')
- grad_first_shift: float32 [1024], P('fsdp')
- grad_second_gain: float32 [1024], P('fsdp')
- grad_second_shift: float32 [1024], P('fsdp')
The draws below stay inside these ranges and needn't reach their ends.
Inputs may be any that keep to these rules, and one draw needn't show every extreme that they name: `segment_ids`: within a sequence the numbers never fall; a segment has 1 to 2048 positions and one has exactly 2048.
All inputs are finite; a program needn't handle non-finite values.
Results may differ from the reference program's by a relative error of at most 0.023.
Values may be sent and summed in bfloat16 or wider, within the bound.
No kernel may reach another device: no remote copies, remote signals or barrier semaphores. Data moves between devices by JAX's collectives and lax.ppermute only.
A program may use at most 192 MiB of HBM per device.

```python
import math
import jax
import jax.numpy as jnp
import numpy as np
from jax import lax

D = 1024
H = 16
HD = 64
FF = 4096
LEN = 4096
NSEQ = 2
SEGMENTS = 32


def levels(own_key, shape, shards, smallest, top_value):
    level, own = 1.0, jax.random.fold_in(own_key, 6)
    for axis_at, shards_of in shards:
        heights = jnp.exp(jax.random.uniform(jax.random.fold_in(own, axis_at), (shards_of,), jnp.float32, smallest / len(shards), top_value / len(shards)))
        level = level * jnp.repeat(heights, shape[axis_at] // shards_of).reshape([-1 if axis == axis_at else 1 for axis in range(len(shape))])
    return level


def length_profile(count, total, limit, slope):
    weights = [(1 << 20) // math.isqrt(grade ** slope) + 1 for grade in range(2, count + 1)]
    surplus, holding = total - limit - (count - 1), [1] * (count - 1)
    while surplus > 0:
        movable = [i for i in range(count - 1) if holding[i] < limit]
        mass, budget = sum([weights[i] for i in movable]), surplus
        for i in movable:
            addition = min(limit - holding[i], max(1, budget * weights[i] // mass), surplus)
            holding[i] = holding[i] + addition
            surplus = surplus - addition
    return np.array([limit] + holding)


def ragged_sizes(key, count, total, most, slope):
    if count == 2:
        one = jax.random.randint(key, (), max(1, total - most), min(most, total - 1) + 1)
        return jnp.stack([one, total - one])
    lengths = jnp.asarray(length_profile(count, total, most, slope), jnp.int32)
    pairs = (count - 1) // 2
    donor, sink = lengths[1:1 + 2 * pairs:2], lengths[2:2 + 2 * pairs:2]
    margin = jnp.minimum(donor - 1, most - sink)
    shifted = jax.random.randint(jax.random.fold_in(key, 1), (pairs,), 0, 1 << 20) % (margin + 1)
    lengths = lengths.at[1:1 + 2 * pairs:2].set(donor - shifted).at[2:2 + 2 * pairs:2].set(sink + shifted)
    return lengths[jax.random.permutation(jax.random.fold_in(key, 2), count)]


def gaussian(own_key, shape, width, bound, shards=(), held_as=jnp.bfloat16):
    values = width * jax.random.normal(own_key, shape, jnp.float32)
    if shards:
        values = values * levels(own_key, shape, shards, -0.22, 0.18)
    return jnp.clip(values, -bound, bound).astype(held_as)


def setup_inputs(seed: int = 0) -> dict:
    splits = jax.random.split(jax.random.key(seed), 17)
    tokens = gaussian(splits[0], (NSEQ, LEN, D), 1.0, 6.0, ((0, 2), (1, 4)))
    cotangent = gaussian(splits[1], (NSEQ, LEN, D), 1.0, 6.0, ((0, 2), (1, 4)))
    segment_ids = jax.vmap(lambda own: jnp.searchsorted(jnp.cumsum(ragged_sizes(own, SEGMENTS, LEN, LEN // 2, 2)), jnp.arange(LEN), side="right"))(jax.random.split(splits[2], NSEQ)).reshape((NSEQ, LEN)).astype(jnp.int32)
    in_weight = gaussian(splits[3], (D, 3, D), (D // 2) ** -0.5, 0.25, ((0, 2), (2, 4)))
    out_weight = gaussian(splits[4], (D, D), (D // 8) ** -0.5, 0.5, ((0, 8),))
    up_weight = gaussian(splits[5], (D, FF), D ** -0.5, 0.1875, ((0, 2), (1, 4)))
    down_weight = gaussian(splits[6], (FF, D), FF ** -0.5, 0.09375, ((0, 8),))
    query_bias = gaussian(splits[7], (D,), 0.5, 3.0, ((0, 8),))
    value_bias = gaussian(splits[8], (D,), 0.5, 3.0, ((0, 8),))
    out_bias = gaussian(splits[9], (D,), 0.5, 3.0, ((0, 2),))
    up_bias = gaussian(splits[10], (FF,), 0.5, 3.0, ((0, 8),))
    down_bias = gaussian(splits[11], (D,), 0.5, 3.0, ((0, 2),))
    first_gain = jnp.clip(1.0 + 0.1 * jax.random.normal(splits[12], (D,), jnp.float32), 0.5, 1.5).astype(jnp.bfloat16)
    first_shift = gaussian(splits[13], (D,), 0.3, 2.0, ((0, 2),))
    second_gain = jnp.clip(1.0 + 0.1 * jax.random.normal(splits[14], (D,), jnp.float32), 0.5, 1.5).astype(jnp.bfloat16)
    second_shift = gaussian(splits[15], (D,), 0.3, 2.0, ((0, 2),))
    return dict(tokens=tokens, cotangent=cotangent, segment_ids=segment_ids, in_weight=in_weight, out_weight=out_weight, up_weight=up_weight, down_weight=down_weight, query_bias=query_bias, value_bias=value_bias, out_bias=out_bias, up_bias=up_bias, down_bias=down_bias, first_gain=first_gain, first_shift=first_shift, second_gain=second_gain, second_shift=second_shift)


@jax.custom_vjp
def low(v):
    return lax.optimization_barrier(v.astype(jnp.bfloat16)).astype(jnp.float32)

@jax.custom_vjp
def low_back(v):
    return v

def low_keep(v):
    return (low(v), None)

def low_pass(kept, grad):
    return (grad,)

def back_keep(v):
    return (v, None)

def back_low(kept, grad):
    return (low(grad),)
low.defvjp(low_keep, low_pass)
low_back.defvjp(back_keep, back_low)

def matmul(left, right):
    return jnp.dot(left, right, precision=lax.Precision.HIGHEST, preferred_element_type=jnp.float32)

def normalize(values, gain, shift):
    center = values - lax.optimization_barrier(jnp.mean(values, axis=-1, keepdims=True))
    spread = lax.optimization_barrier(jnp.mean(center * center, axis=-1, keepdims=True))
    return center * lax.rsqrt(spread + 1e-05) * gain + shift

def gelu(values):
    return 0.5 * values * (1.0 + jnp.tanh(0.7978845608028654 * (values + 0.044715 * values * values * values)))

def attention(query, keys, values, segments):
    length = query.shape[0]
    block = min(512, length)
    positions = jnp.arange(length).astype(jnp.int32)

    def one_block(index):
        start = (index * block).astype(jnp.int32)
        rows = lax.dynamic_slice_in_dim(query, start, block, 0)
        row_groups = lax.dynamic_slice_in_dim(segments, start, block, 0)
        row_positions = start + jnp.arange(block).astype(jnp.int32)
        scores = low_back(0.125 * jnp.einsum('qhd,khd->hqk', rows, keys, precision=lax.Precision.HIGHEST))
        allowed = (row_groups[:, None] == segments[None, :]) & (positions[None, :] <= row_positions[:, None])
        masked = jnp.where(allowed[None], scores, -1e+30)
        largest = lax.optimization_barrier(jnp.max(masked, axis=-1, keepdims=True))
        raised = jnp.where(allowed[None], jnp.exp(masked - largest), 0.0)
        weights = low(raised / lax.optimization_barrier(jnp.sum(raised, axis=-1, keepdims=True)))
        return jnp.einsum('hqk,khd->qhd', weights, values, precision=lax.Precision.HIGHEST)
    blocks = lax.map(jax.checkpoint(one_block), jnp.arange(length // block).astype(jnp.int32))
    return blocks.reshape(length, H * HD)

def forward(weights_all, inputs, segments):
    in_w, out_w, up_w, down_w, query_add, value_add, out_add, up_add, down_add, gain_one, shift_one, gain_two, shift_two = weights_all
    first = low(normalize(inputs, gain_one, shift_one))
    mixed = matmul(first, in_w.reshape(D, 3 * D))
    query = low(low_back(mixed[:, :D] + query_add))
    keys = low(low_back(mixed[:, D:2 * D]))
    values = low(low_back(mixed[:, 2 * D:] + value_add))
    heads = attention(query.reshape(LEN, H, HD), keys.reshape(LEN, H, HD), values.reshape(LEN, H, HD), segments)
    heads = low(low_back(heads))
    attended = low_back(matmul(heads, out_w) + out_add)
    middle = inputs + attended
    second = low(normalize(middle, gain_two, shift_two))
    hidden = low(gelu(low_back(matmul(second, up_w) + up_add)))
    return middle + matmul(hidden, down_w) + down_add

def reference(tokens, cotangent, segment_ids, in_weight, out_weight, up_weight, down_weight, query_bias, value_bias, out_bias, up_bias, down_bias, first_gain, first_shift, second_gain, second_shift):
    weights_all = tuple((piece.astype(jnp.float32) for piece in (in_weight, out_weight, up_weight, down_weight, query_bias, value_bias, out_bias, up_bias, down_bias, first_gain, first_shift, second_gain, second_shift)))

    def one_sequence(totals, inputs_seq):
        token_rows, cot_rows, group_rows = inputs_seq
        output, pullback = jax.vjp(lambda params, rows: forward(params, rows, group_rows), weights_all, token_rows.astype(jnp.float32))
        grads, row_grad = pullback(cot_rows.astype(jnp.float32))
        totals = jax.tree.map(lambda left, right: left + right, totals, grads)
        return (totals, (output.astype(jnp.bfloat16), row_grad))
    zeros = jax.tree.map(jnp.zeros_like, weights_all)
    totals, (outputs, input_grads) = lax.scan(one_sequence, zeros, (tokens, cotangent, segment_ids))
    return (outputs, input_grads, totals[0], totals[1], totals[2], totals[3], totals[4], totals[5], totals[6], totals[7], totals[8], totals[9], totals[10], totals[11], totals[12])
```

```python
import functools

import jax
import jax.numpy as jnp
from jax import lax
from jax.experimental import pallas as pl
from jax.experimental.pallas import tpu as pltpu
from jax.sharding import PartitionSpec as P

HD = 64
RATE = 0.125 * 1.4426950408889634
BQ = 256
BK = 256


def head_rows(block, head):
    rows = lax.broadcasted_iota(jnp.int32, block.shape, 0)
    return jnp.where((rows >= head * HD) & (rows < (head + 1) * HD), block, jnp.zeros_like(block))


def head_lanes(block, head):
    lanes = lax.broadcasted_iota(jnp.int32, block.shape, 1)
    return jnp.where((lanes >= head * HD) & (lanes < (head + 1) * HD), block, jnp.zeros_like(block))


def key_mask(starts, key_base, own):
    shape = (BK, BQ)
    keys = lax.broadcasted_iota(jnp.int32, shape, 0)
    allowed = keys >= starts - key_base
    if own:
        allowed = allowed & (keys <= lax.broadcasted_iota(jnp.int32, shape, 1))
    return allowed


def forward_kernel(base, first, last, low_ref, *refs):
    q_ref, kv_ref, start_ref = refs[:3]
    refs = refs[3:]
    if not first:
        acc_in, stat_in = refs[:2]
        refs = refs[2:]
    if last:
        heads_ref, lse_ref, value_t = refs
    else:
        acc_out, stat_out, value_t = refs
    heads = q_ref.shape[1] // HD
    width = heads * HD
    blocks = kv_ref.shape[0] // BK
    index = pl.program_id(0)

    @pl.when(index == 0)
    def _():
        for block in range(blocks):
            value_t[:, block * BK : (block + 1) * BK] = jnp.transpose(
                kv_ref[block * BK : (block + 1) * BK, width:]
            )

    query_t = jnp.transpose(q_ref[...])
    starts = start_ref[0:1, :]
    masked_query = [head_rows(query_t, head) for head in range(heads)]

    def step(key_block, state, own):
        offset = pl.multiple_of(key_block * BK, BK)
        keys = kv_ref[pl.ds(offset, BK), :width]
        values = value_t[:, pl.ds(offset, BK)]
        allowed = key_mask(starts, base + offset, own)
        result = []
        for head in range(heads):
            largest, total, summed = state[head]
            scores = jnp.dot(keys, masked_query[head], preferred_element_type=jnp.float32)
            scores = jnp.where(allowed, scores, -1e30)
            block_largest = jnp.max(scores, axis=0, keepdims=True)
            new_largest = block_largest if largest is None else jnp.maximum(largest, block_largest)
            raised = jnp.exp2((scores - new_largest) * RATE)
            block_total = jnp.sum(raised, axis=0, keepdims=True)
            product = jnp.dot(
                values[head * HD : (head + 1) * HD],
                raised.astype(jnp.bfloat16),
                preferred_element_type=jnp.float32,
            )
            if largest is None:
                result.append((new_largest, block_total, product))
            else:
                factor = jnp.exp2((largest - new_largest) * RATE)
                result.append((new_largest, total * factor + block_total, summed * factor + product))
        return tuple(result)

    low = low_ref[index]
    if first:
        state = step(index, ((None, None, None),) * heads, True)
        state = lax.fori_loop(
            0, index - low, lambda i, kept: step(index - 1 - i, kept, False), state
        )
    else:
        state = tuple(
            (
                stat_in[head : head + 1, :],
                stat_in[heads + head : heads + head + 1, :],
                acc_in[head * HD : (head + 1) * HD, :],
            )
            for head in range(heads)
        )
        state = lax.fori_loop(low, blocks, lambda i, kept: step(i, kept, False), state)
    if last:
        parts, sums = [], []
        for largest, total, summed in state:
            parts.append(summed * (1.0 / total))
            sums.append(largest * RATE + jnp.log2(total))
        heads_ref[...] = jnp.transpose(jnp.concatenate(parts, axis=0).astype(jnp.bfloat16))
        lse_ref[...] = jnp.concatenate(sums + sums, axis=0)
    else:
        acc_out[...] = jnp.concatenate([piece[2] for piece in state], axis=0)
        stat_out[...] = jnp.concatenate(
            [piece[0] for piece in state] + [piece[1] for piece in state], axis=0
        )


def row_block(rows):
    return pl.BlockSpec((rows, BQ), lambda i, low: (0, i))


def forward_shard(base, first, last, low, query, pair, starts, state):
    rows, width = query.shape
    heads = width // HD
    stats = 2 * heads
    in_specs = [
        pl.BlockSpec((BQ, width), lambda i, low: (i, 0)),
        pl.BlockSpec(pair.shape, lambda i, low: (0, 0)),
        row_block(starts.shape[0]),
    ]
    operands = [query, pair, starts]
    if not first:
        in_specs += [row_block(width), row_block(stats)]
        operands += list(state)
    if last:
        out_specs = [pl.BlockSpec((BQ, width), lambda i, low: (i, 0)), row_block(stats)]
        out_shape = [
            jax.ShapeDtypeStruct((rows, width), jnp.bfloat16),
            jax.ShapeDtypeStruct((stats, rows), jnp.float32),
        ]
    else:
        out_specs = [row_block(width), row_block(stats)]
        out_shape = [
            jax.ShapeDtypeStruct((width, rows), jnp.float32),
            jax.ShapeDtypeStruct((stats, rows), jnp.float32),
        ]
    return pl.pallas_call(
        functools.partial(forward_kernel, base, first, last),
        grid_spec=pltpu.PrefetchScalarGridSpec(
            num_scalar_prefetch=1,
            grid=(rows // BQ,),
            in_specs=in_specs,
            out_specs=out_specs,
            scratch_shapes=[pltpu.VMEM((width, pair.shape[0]), jnp.bfloat16)],
        ),
        out_shape=out_shape,
        cost_estimate=pl.CostEstimate(
            flops=4 * rows * rows * width, bytes_accessed=4 * rows * width * 4, transcendentals=0
        ),
        name="attend_own" if first else "attend_last" if last else "attend_mid",
    )(low, *operands)


def backward_kernel(base, own, first, low_ref, *refs):
    q_ref, do_ref, heads_ref, kv_ref, start_ref, lse_ref = refs[:6]
    refs = refs[6:]
    if not first:
        dq_in = refs[0]
        refs = refs[1:]
    dq_out, dkv_out, key_t, dk_acc, dv_acc = refs
    heads = q_ref.shape[1] // HD
    width = heads * HD
    blocks = kv_ref.shape[0] // BK
    index = pl.program_id(0)

    @pl.when(index == 0)
    def _():
        for block in range(blocks):
            key_t[:, block * BK : (block + 1) * BK] = jnp.transpose(
                kv_ref[block * BK : (block + 1) * BK, :width]
            )
        dk_acc[...] = jnp.zeros_like(dk_acc)
        dv_acc[...] = jnp.zeros_like(dv_acc)

    low = low_ref[index]
    high = index + 1 if own else blocks
    if first:
        dq_out[...] = jnp.zeros_like(dq_out)
    else:
        dq_out[...] = dq_in[...]

    @pl.when(low < high)
    def _():
        query = q_ref[...]
        grad = do_ref[...]
        query_t = jnp.transpose(query)
        grad_t = jnp.transpose(grad)
        heads_t = jnp.transpose(heads_ref[...])
        weighted = grad_t.astype(jnp.float32) * heads_t.astype(jnp.float32)
        starts = start_ref[0:1, :]

        def step(key_block, own_block):
            offset = pl.multiple_of(key_block * BK, BK)
            keys = kv_ref[pl.ds(offset, BK), :width]
            values = kv_ref[pl.ds(offset, BK), width:]
            allowed = key_mask(starts, base + offset, own_block)
            dk = dk_acc[pl.ds(offset, BK), :]
            dv = dv_acc[pl.ds(offset, BK), :]
            for head in range(heads):
                rows = slice(head * HD, (head + 1) * HD)
                inner = jnp.sum(weighted[rows], axis=0, keepdims=True)
                scores = jnp.dot(keys, head_rows(query_t, head), preferred_element_type=jnp.float32)
                weights = jnp.exp2(
                    jnp.where(allowed, scores * RATE - lse_ref[head : head + 1, :], -1e30)
                )
                products = jnp.dot(values, head_rows(grad_t, head), preferred_element_type=jnp.float32)
                grad_scores = (weights * (products - inner)).astype(jnp.bfloat16)
                dv = dv + jnp.dot(
                    weights.astype(jnp.bfloat16), head_lanes(grad, head), preferred_element_type=jnp.float32
                )
                dk = dk + jnp.dot(grad_scores, head_lanes(query, head), preferred_element_type=jnp.float32)
                dq_out[rows, :] += 0.125 * jnp.dot(
                    key_t[rows, pl.ds(offset, BK)], grad_scores, preferred_element_type=jnp.float32
                )
            dk_acc[pl.ds(offset, BK), :] = dk
            dv_acc[pl.ds(offset, BK), :] = dv

        if own:
            step(index, True)
        top = index if own else blocks

        def body(i, carry):
            step(i, False)
            return carry

        lax.fori_loop(low, top, body, 0)

    @pl.when(index == pl.num_programs(0) - 1)
    def _():
        dkv_out[:, :width] = (0.125 * dk_acc[...]).astype(jnp.bfloat16)
        dkv_out[:, width:] = dv_acc[...].astype(jnp.bfloat16)


def backward_shard(base, own, first, low, query, grad, heads_value, pair, starts, lse, state):
    rows, width = query.shape
    by_rows = pl.BlockSpec((BQ, width), lambda i, low: (i, 0))
    in_specs = [
        by_rows,
        by_rows,
        by_rows,
        pl.BlockSpec(pair.shape, lambda i, low: (0, 0)),
        row_block(starts.shape[0]),
        row_block(lse.shape[0]),
    ]
    operands = [query, grad, heads_value, pair, starts, lse]
    if not first:
        in_specs.append(row_block(width))
        operands.append(state)
    return pl.pallas_call(
        functools.partial(backward_kernel, base, own, first),
        grid_spec=pltpu.PrefetchScalarGridSpec(
            num_scalar_prefetch=1,
            grid=(rows // BQ,),
            in_specs=in_specs,
            out_specs=[row_block(width), pl.BlockSpec(pair.shape, lambda i, low: (0, 0))],
            scratch_shapes=[
                pltpu.VMEM((width, pair.shape[0]), jnp.bfloat16),
                pltpu.VMEM((pair.shape[0], width), jnp.float32),
                pltpu.VMEM((pair.shape[0], width), jnp.float32),
            ],
        ),
        out_shape=[
            jax.ShapeDtypeStruct((width, rows), jnp.float32),
            jax.ShapeDtypeStruct(pair.shape, jnp.bfloat16),
        ],
        cost_estimate=pl.CostEstimate(
            flops=10 * rows * rows * width, bytes_accessed=4 * rows * width * 4, transcendentals=0
        ),
        name="attend_back_own" if own else "attend_back",
    )(low, *operands)


def dot(left, right):
    return jnp.dot(left, right, preferred_element_type=jnp.float32)


def transpose_dot(left, right):
    return lax.dot_general(
        left, right, (((0,), (0,)), ((), ())), preferred_element_type=jnp.float32
    )


def dot_rows(left, right):
    return lax.dot_general(
        left, right, (((1,), (1,)), ((), ())), preferred_element_type=jnp.float32
    )


def narrow(values):
    return values.astype(jnp.bfloat16)


def wide(values):
    return values.astype(jnp.float32)


def normal_parts(values):
    center = values - jnp.mean(values, axis=-1, keepdims=True)
    spread = jnp.mean(center * center, axis=-1, keepdims=True)
    scale = lax.rsqrt(spread + 1e-05)
    return center * scale, scale


def normal_back(grad, gain, ready, scale):
    grad_ready = grad * gain
    first = jnp.mean(grad_ready, axis=-1, keepdims=True)
    second = jnp.mean(grad_ready * ready, axis=-1, keepdims=True)
    return scale * (grad_ready - first - ready * second)


def gelu_pair(values):
    square = values * values
    bend = jnp.tanh(0.7978845608028654 * values * (1.0 + 0.044715 * square))
    half = 0.5 * (1.0 + bend)
    slope = half + 0.5 * values * (1.0 - bend * bend) * (
        0.7978845608028654 * (1.0 + 0.134145 * square)
    )
    return values * half, slope


def swap_y(values):
    return lax.ppermute(values, "fsdp", [(0, 1), (1, 0)])


def swap_core(values):
    return lax.ppermute(values, "tp", [(0, 1), (1, 0), (2, 3), (3, 2)])


def swap_x(values):
    return lax.ppermute(values, "tp", [(0, 2), (2, 0), (1, 3), (3, 1)])


def to_right(values):
    size = lax.axis_size("ctx")
    return lax.ppermute(values, "ctx", [(i, i + 1) for i in range(size - 1)])


def to_left(values):
    size = lax.axis_size("ctx")
    return lax.ppermute(values, "ctx", [(i + 1, i) for i in range(size - 1)])


def in_order(bit, own, other, axis=0):
    return jnp.where(
        bit == 0,
        jnp.concatenate([own, other], axis=axis),
        jnp.concatenate([other, own], axis=axis),
    )


def gather(values, axis=0):
    if lax.axis_size("fsdp") == 2:
        return in_order(lax.axis_index("fsdp"), values, swap_y(values), axis)
    return lax.all_gather(values, "fsdp", axis=axis, tiled=True)


def rows_at(values, index, count):
    return lax.dynamic_slice_in_dim(values, index * count, count, 0)


def scatter(values):
    if lax.axis_size("fsdp") == 2:
        half = values.shape[0] // 2
        place = lax.axis_index("fsdp")
        sent = narrow(rows_at(values, 1 - place, half))
        return narrow(rows_at(values, place, half) + wide(swap_y(sent)))
    return lax.psum_scatter(narrow(values), "fsdp", scatter_dimension=0, tiled=True)


def sum_context(values):
    if lax.axis_size("ctx") == 4:
        place = lax.axis_index("ctx")
        inward = lax.ppermute(values, "ctx", [(0, 1), (3, 2)])
        joined = narrow(wide(values) + wide(inward))
        across = lax.ppermute(joined, "ctx", [(1, 2), (2, 1)])
        total = narrow(wide(joined) + wide(across))
        outward = lax.ppermute(total, "ctx", [(1, 0), (2, 3)])
        return jnp.where((place == 0) | (place == 3), wide(outward), wide(total))
    return wide(lax.psum(values, "ctx"))


def sum_small(values):
    if lax.axis_size("fsdp") == 2 and lax.axis_size("ctx") == 4:
        values = values + swap_y(values)
        values = values + lax.ppermute(values, "ctx", [(0, 1), (1, 0), (2, 3), (3, 2)])
        return values + lax.ppermute(values, "ctx", [(0, 2), (2, 0), (1, 3), (3, 1)])
    return lax.psum(values, ("fsdp", "ctx"))


GROUPS = 1


def per_device(
    tokens,
    cotangent,
    segment_ids,
    in_weight,
    out_weight,
    up_weight,
    down_weight,
    query_bias,
    value_bias,
    out_bias,
    up_bias,
    down_bias,
    first_gain,
    first_shift,
    second_gain,
    second_shift,
):
    rows, features = tokens.shape[1:]
    halo = lax.axis_size("ctx") // 2
    half, quarter = rows // 2, rows // 4
    rank = lax.axis_index("tp")
    x_bit, core_bit = rank // 2, rank % 2
    place = 2 * core_bit + x_bit
    shards = lax.axis_size("fsdp")

    vectors = [
        query_bias,
        value_bias,
        up_bias,
        out_bias,
        down_bias,
        first_gain,
        first_shift,
        second_gain,
        second_shift,
    ]
    packed = jnp.concatenate(vectors)
    packed = gather(packed).reshape(shards, packed.shape[0])
    whole, at = [], 0
    for vector in vectors:
        size = vector.shape[0]
        whole.append(wide(packed[:, at : at + size].reshape(1, shards * size)))
        at += size
    query_add, value_add, up_add, out_add, down_add, gain_one, shift_one, gain_two, shift_two = whole

    inputs = tokens[0]
    groups = segment_ids[0]
    mark = jnp.broadcast_to(narrow(groups.astype(jnp.float32) + 1.0)[None], (16, rows))
    travelling = jnp.concatenate([rows_at(inputs, place, quarter), mark], axis=0)
    before = []
    for _ in range(halo):
        travelling = to_right(travelling)
        before.append(travelling)

    width = in_weight.shape[2]
    in_full = gather(jnp.transpose(in_weight, (1, 0, 2)), 1)
    query_weight = in_full[0]
    pair_weight = jnp.concatenate([in_full[1], in_full[2]], axis=1)
    out_full = gather(out_weight)
    up_full = gather(up_weight)
    down_full = gather(down_weight)

    def first_of(values):
        return narrow(normal_parts(wide(values))[0] * gain_one + shift_one)

    pair_add = jnp.concatenate([jnp.zeros_like(value_add), value_add], axis=1)
    firsts, pairs, marks = [], [], []
    own_first = first_of(inputs)
    firsts.append(own_first)
    query = narrow(dot(own_first, query_weight) + query_add)
    pairs.append(narrow(dot(own_first, pair_weight) + pair_add))
    marks.append(groups + 1)
    for piece in before:
        normal = first_of(piece[:quarter])
        mine = in_order(x_bit, normal, swap_x(normal))
        block = in_order(core_bit, mine, swap_core(mine))
        firsts.append(block)
        pairs.append(narrow(dot(block, pair_weight) + pair_add))
        marks.append(piece[quarter].astype(jnp.int32))
    firsts, pairs, marks = firsts[::-1], pairs[::-1], marks[::-1]

    window = jnp.concatenate(marks)
    start = jnp.sum(window[None, :] < (groups + 1)[:, None], axis=1, dtype=jnp.int32)
    blocks = rows // BK
    lows = start[::BQ] // BK
    lows = [jnp.clip(lows - shard * blocks, 0, blocks) for shard in range(halo + 1)]
    starts = jnp.broadcast_to(start[None], (8, rows))
    state = None
    for count, shard in enumerate([halo] + list(range(halo - 1, -1, -1))):
        state = forward_shard(
            shard * rows, count == 0, count == halo, lows[shard], query, pairs[shard], starts, state
        )
    heads, logsum = state

    def halves(values):
        return rows_at(values, core_bit, half), rows_at(values, 1 - core_bit, half)

    def join(keep, sent):
        return narrow(keep + wide(swap_core(narrow(sent))))

    def add_x(part):
        return wide(part) + wide(swap_x(part))

    heads_own, heads_other = halves(heads)
    inputs_own = halves(inputs)[0]
    cot_own, cot_other = halves(cotangent[0])
    step = half // GROUPS
    middle, ready_two, scale_two, second, cot, grad_hidden = [], [], [], [], [], []
    for group in range(GROUPS):
        span = slice(group * step, (group + 1) * step)
        cot.append(jnp.concatenate([cot_own[span], cot_other[span]], axis=0))
        grad_hidden.append(dot_rows(cot[group], down_full))
    for group in range(GROUPS):
        span = slice(group * step, (group + 1) * step)
        part = join(dot(heads_own[span], out_full), dot(heads_other[span], out_full))
        middle.append(wide(inputs_own[span]) + add_x(part) + out_add)
        ready, scale = normal_parts(middle[group])
        ready_two.append(ready)
        scale_two.append(scale)
        normal = narrow(ready * gain_two + shift_two)
        second.append(jnp.concatenate([normal, swap_core(normal)], axis=0))

    hidden, grad_pre, grad_part = [], [], []
    for group in range(GROUPS):
        value, slope = gelu_pair(dot(second[group], up_full) + up_add)
        hidden.append(narrow(value))
        grad_pre.append(narrow(grad_hidden[group] * slope))
        grad_part.append(dot_rows(grad_pre[group], up_full))

    grad_middle, attended, sums_two = [], [], []
    for group in range(GROUPS):
        grad_second = add_x(join(grad_part[group][:step], grad_part[group][step:]))
        cot_here = wide(cot[group][:step])
        back = normal_back(grad_second, gain_two, ready_two[group], scale_two[group])
        grad_middle.append(cot_here + back)
        attended.append(narrow(grad_middle[group]))
        sums_two.append(
            [
                jnp.sum(wide(attended[group]), axis=0),
                jnp.sum(cot_here, axis=0),
                jnp.sum(grad_second * ready_two[group], axis=0),
                jnp.sum(grad_second, axis=0),
            ]
        )
    other_attended = [swap_core(piece) for piece in attended]
    grad_attended = in_order(
        core_bit, jnp.concatenate(attended, axis=0), jnp.concatenate(other_attended, axis=0)
    )
    grad_heads = narrow(dot_rows(grad_attended, out_full))

    grad_query, grad_pairs = None, []
    for shard in range(halo + 1):
        grad_query, grad_pair = backward_shard(
            shard * rows,
            shard == halo,
            shard == 0,
            lows[shard],
            query,
            grad_heads,
            heads,
            pairs[shard],
            starts,
            logsum,
            grad_query,
        )
        grad_pairs.append(grad_pair)
    grad_query = narrow(jnp.transpose(grad_query))

    total = None
    for shard in range(halo + 1):
        own, other = halves(grad_pairs[shard])
        own, other = dot_rows(own, pair_weight), dot_rows(other, pair_weight)
        if shard == halo:
            own_query, other_query = halves(grad_query)
            own = own + dot_rows(own_query, query_weight)
            other = other + dot_rows(other_query, query_weight)
        part = join(own, other)
        there = swap_x(rows_at(part, 1 - x_bit, quarter))
        here = wide(rows_at(part, x_bit, quarter)) + wide(there)
        if total is not None:
            here = here + wide(to_left(total))
        total = narrow(here)
    grad_first = wide(in_order(x_bit, total, swap_x(total)))
    ready, scale = normal_parts(wide(inputs_own))
    grad_input = jnp.concatenate(grad_middle, axis=0) + normal_back(
        grad_first, gain_one, ready, scale
    )
    grad_input = in_order(core_bit, grad_input, swap_core(grad_input))
    sums_one = [jnp.sum(grad_first * ready, axis=0), jnp.sum(grad_first, axis=0)]

    result = []
    for group in range(GROUPS):
        product = dot(hidden[group], down_full)
        piece = middle[group] + add_x(join(product[:step], product[step:])) + down_add
        result.append(narrow(piece))
    result = jnp.concatenate(result, axis=0)
    result = in_order(core_bit, result, swap_core(result))

    def add_all(terms):
        return functools.reduce(lambda left, right: left + right, terms)

    grad_down = sum_context(
        scatter(add_all([transpose_dot(hidden[i], cot[i]) for i in range(GROUPS)]))
    )
    grad_up = sum_context(
        scatter(add_all([transpose_dot(second[i], grad_pre[i]) for i in range(GROUPS)]))
    )
    grad_out = sum_context(scatter(transpose_dot(heads, grad_attended)))
    grad_pair = add_all([transpose_dot(firsts[i], grad_pairs[i]) for i in range(halo + 1)])
    grad_in = jnp.concatenate([transpose_dot(firsts[halo], grad_query), grad_pair], axis=1)
    grad_in = sum_context(scatter(grad_in))
    grad_in = jnp.transpose(
        jnp.stack([grad_in[:, :width], grad_in[:, width : 2 * width], grad_in[:, 2 * width :]]),
        (1, 0, 2),
    )

    shared = jnp.stack(
        [add_all([piece[i] for piece in sums_two]) for i in range(4)] + sums_one
    ).reshape(-1)
    shared = shared + swap_core(shared)
    local = jnp.concatenate(
        [
            add_all([jnp.sum(wide(piece), axis=0) for piece in grad_pre]),
            jnp.sum(wide(grad_query), axis=0),
            add_all([jnp.sum(wide(piece[:, width:]), axis=0) for piece in grad_pairs]),
        ]
    )
    sums = sum_small(jnp.concatenate([shared, local]).reshape(-1, 128)).reshape(-1)
    mine, at = [], 0
    for size in [features] * 6 + [up_add.shape[1], width, width]:
        piece = sums[at : at + size].reshape(shards, size // shards)
        mine.append(lax.dynamic_index_in_dim(piece, lax.axis_index("fsdp"), 0, keepdims=False))
        at += size
    return (
        result[None],
        grad_input[None],
        grad_in,
        grad_out,
        grad_up,
        grad_down,
        mine[7],
        mine[8],
        mine[0],
        mine[6],
        mine[1],
        mine[4],
        mine[5],
        mine[2],
        mine[3],
    )


def solution(mesh):
    placed = (
        P("fsdp", "ctx", None),
        P("fsdp", "ctx", None),
        P("fsdp", "ctx"),
        P("fsdp", None, "tp"),
        P(("tp", "fsdp"), None),
        P("fsdp", "tp"),
        P(("tp", "fsdp"), None),
        P(("tp", "fsdp")),
        P(("tp", "fsdp")),
        P("fsdp"),
        P(("tp", "fsdp")),
        P("fsdp"),
        P("fsdp"),
        P("fsdp"),
        P("fsdp"),
        P("fsdp"),
    )
    return jax.shard_map(
        per_device,
        mesh=mesh,
        in_specs=placed,
        out_specs=(
            P("fsdp", "ctx", None),
            P("fsdp", "ctx", None),
            P("fsdp", None, "tp"),
            P(("tp", "fsdp"), None),
            P("fsdp", "tp"),
            P(("tp", "fsdp"), None),
            P(("tp", "fsdp")),
            P(("tp", "fsdp")),
            P("fsdp"),
            P(("tp", "fsdp")),
            P("fsdp"),
            P("fsdp"),
            P("fsdp"),
            P("fsdp"),
            P("fsdp"),
        ),
        check_vma=False,
    )
```
